256 devices in a mesh: dp: 64 (over y, z, core), tensor: 4 (over x).
Axes of the slice: x: 4, y: 4, z: 8, core: 2. Of those that a mesh axis runs over, the one named last changes fastest.
Arguments:
- activations: bfloat16 [32768, 8192], P('dp', 'tensor'), may hold values from -2000 to 2000
- norm_gain: float32 [8192], replicated, may hold values from 0.5 to 12
- w_query: bfloat16 [8192, 4096], P('dp', 'tensor'), may hold values from -0.0625 to 0.0625
- w_key: bfloat16 [8192, 512], P('dp', 'tensor'), may hold values from -0.0625 to 0.0625
- w_value: bfloat16 [8192, 512], P('dp', 'tensor'), may hold values from -0.0625 to 0.0625
- lengths: int32 [128], replicated, may hold values from 128 to 256
- languages: int32 [128], replicated, may hold values from 0 to 29
- lang_caps: int32 [30], replicated, may hold values from 128 to 256
- dest_shard: int32 [128], replicated, may hold values from 0 to 63, as said below
Outputs:
- attended: bfloat16 [32768, 4096], P('dp', 'tensor')
The draws below stay inside these ranges and needn't reach their ends.
Inputs may be any that keep to these rules, and one draw needn't show every extreme that they name: `dest_shard`: every data shard receives exactly 2 documents.
All inputs are finite; a program needn't handle non-finite values.
Results may differ from the reference program's by a relative error of at most 0.007.
The reference program's roundings to bfloat16 on the way count: a program that leaves them out, or rounds other values in their place, can miss the bound.
Values may be sent and summed in bfloat16 or wider, within the bound.
A program may use at most 128 MiB of HBM per device.

```python
import math
import jax
import jax.numpy as jnp
from jax import lax

D = 8192
HEAD_WIDTH = 128
QUERY_HEADS = 32
KEY_VALUE_HEADS = 4
LANGS = 30
DOCUMENT_ROWS = 256
DOCUMENTS_SHARD = 2
TOKENS = 32768
DOCS = 128
QW = 4096
KW = 512
N_DP = 64


def plan_tables(key):
    lang_used = min(LANGS, DOCS)
    half_most = max(1, DOCUMENT_ROWS // 2)
    doc_range = jnp.arange(DOCS)
    order_values = jax.random.permutation(jax.random.fold_in(key, 11), DOCS)
    destination = order_values // DOCUMENTS_SHARD
    language_values = jax.random.permutation(jax.random.fold_in(key, 12), DOCS) % lang_used
    length_values = jax.random.randint(jax.random.fold_in(key, 13), (DOCS,), half_most, DOCUMENT_ROWS + 1)
    picked = jax.random.randint(jax.random.fold_in(key, 14), (), 0, DOCS)
    second = (picked + 1 + jax.random.randint(jax.random.fold_in(key, 15), (), 0, DOCS - 1)) % DOCS
    length_values = jnp.where(doc_range == picked, DOCUMENT_ROWS, length_values)
    length_values = jnp.where(doc_range == second, half_most, length_values)
    full_language = language_values[picked]
    low_language = (full_language + 1 + jax.random.randint(jax.random.fold_in(key, 16), (), 0, lang_used - 1)) % lang_used
    lang_range = jnp.arange(LANGS)
    cap_values = jax.random.randint(jax.random.fold_in(key, 17), (LANGS,), half_most, DOCUMENT_ROWS + 1)
    cap_values = jnp.where(lang_range == low_language, half_most, cap_values)
    cap_values = jnp.where(lang_range == full_language, DOCUMENT_ROWS, cap_values)
    return (destination.astype(jnp.int32), length_values.astype(jnp.int32), language_values.astype(jnp.int32), cap_values.astype(jnp.int32))


def draw_dest_shard(key, part):
    return plan_tables(key)[0]


def draw_lengths(key, part):
    return plan_tables(key)[1]


def draw_languages(key, part):
    return plan_tables(key)[2]


def draw_lang_caps(key, part):
    return plan_tables(key)[3]


def draw_activations(key, part):
    column_scale = jnp.exp(jax.random.uniform(jax.random.fold_in(key, 3), (1, D), jnp.float32, 0.0, math.log(10.0)))
    base = jax.random.truncated_normal(jax.random.fold_in(key, 1), -6.0, 6.0, (TOKENS, D), jnp.float32)
    row_scale = jnp.exp(jax.random.uniform(jax.random.fold_in(key, 2), (TOKENS, 1), jnp.float32, 0.0, math.log(10.0)))
    return (base * row_scale * column_scale).astype(jnp.bfloat16)


def draw_norm_gain(key, part):
    low_end, high_end = (math.log(0.5), math.log(2.0))
    return jnp.exp(jax.random.uniform(key, (D,), jnp.float32, low_end, high_end))


def levels(stream_key, dims, shards, smallest, high):
    level = 1.0
    for axis_at, shards_of in shards:
        heights = jax.random.uniform(jax.random.fold_in(jax.random.fold_in(stream_key, 6), axis_at), (shards_of,), jnp.float32, smallest / len(shards), high / len(shards))
        level = level * jnp.repeat(jnp.exp(heights), dims[axis_at] // shards_of).reshape((-1,) + (1,) * (len(dims) - 1 - axis_at))
    return level


def centred(own_key, dims, scale, reach, shards=(), held_as=jnp.bfloat16):
    factor_of = levels(own_key, dims, shards, -0.22, 0.18) if shards else 1.0
    entries = jax.random.normal(own_key, dims, jnp.float32) * scale * factor_of
    return jnp.minimum(jnp.maximum(entries, -reach), reach).astype(held_as)


def setup_inputs(seed: int = 0) -> dict:
    arg_keys = jax.random.split(jax.random.key(seed), 10)
    activations = draw_activations(jax.random.fold_in(arg_keys[9], 71), 0)
    norm_gain = draw_norm_gain(jax.random.fold_in(arg_keys[9], 71), 0)
    w_query = centred(arg_keys[2], (D, QW), D ** -0.5, 0.0625, ((0, 64), (1, 4)))
    w_key = centred(arg_keys[3], (D, KW), D ** -0.5, 0.0625, ((0, 64), (1, 4)))
    w_value = centred(arg_keys[4], (D, KW), D ** -0.5, 0.0625, ((0, 64), (1, 4)))
    lengths = draw_lengths(jax.random.fold_in(arg_keys[9], 71), 0)
    languages = draw_languages(jax.random.fold_in(arg_keys[9], 71), 0)
    lang_caps = draw_lang_caps(jax.random.fold_in(arg_keys[9], 71), 0)
    dest_shard = draw_dest_shard(jax.random.fold_in(arg_keys[9], 71), 0)
    return dict(activations=activations, norm_gain=norm_gain, w_query=w_query, w_key=w_key, w_value=w_value, lengths=lengths, languages=languages, lang_caps=lang_caps, dest_shard=dest_shard)


rope_base = 500000.0
norm_eps = 1e-05

def rotary_embedding(vectors, token_positions):
    half_width = vectors.shape[-1] // 2
    steps_range = jnp.arange(half_width, dtype=jnp.float32)
    frequency = jnp.exp(steps_range * (-2.0 * math.log(rope_base) / vectors.shape[-1]))
    angles = token_positions[..., None, None] * frequency
    cosine = jnp.cos(angles)
    sine_table = jnp.sin(angles)
    first_half = vectors[..., :half_width]
    second_half = vectors[..., half_width:]
    return jnp.concatenate([first_half * cosine - second_half * sine_table, second_half * cosine + first_half * sine_table], axis=-1)

def reference(activations, norm_gain, w_query, w_key, w_value, lengths, languages, lang_caps, dest_shard):
    capped = jnp.minimum(lengths, lang_caps[languages]).astype(jnp.int32)
    heads_per_group = QUERY_HEADS // KEY_VALUE_HEADS
    rows_peer = DOCUMENT_ROWS // N_DP
    by_doc = activations.reshape(N_DP, DOCS, rows_peer, D).transpose(1, 2, 0, 3)
    by_doc = by_doc.reshape(DOCS // DOCUMENTS_SHARD, DOCUMENTS_SHARD * DOCUMENT_ROWS, D)

    def per_block(operands):
        block_rows, block_capped = operands
        widened = block_rows.astype(jnp.float32)
        row_scale = lax.rsqrt(lax.optimization_barrier(jnp.mean(widened * widened, axis=1, keepdims=True)) + norm_eps)
        normed = (widened * row_scale * norm_gain).astype(jnp.bfloat16)
        query = jnp.dot(normed, w_query, preferred_element_type=jnp.float32)
        key_portion = jnp.dot(normed, w_key, preferred_element_type=jnp.float32)
        value_portion = jnp.dot(normed, w_value, preferred_element_type=jnp.float32)
        token_positions = jnp.arange(DOCUMENT_ROWS, dtype=jnp.float32)[None, :]
        query_head_rows = rotary_embedding(query.reshape(DOCUMENTS_SHARD, DOCUMENT_ROWS, QUERY_HEADS, HEAD_WIDTH), token_positions).astype(jnp.bfloat16)
        key_head_rows = rotary_embedding(key_portion.reshape(DOCUMENTS_SHARD, DOCUMENT_ROWS, KEY_VALUE_HEADS, HEAD_WIDTH), token_positions).astype(jnp.bfloat16)
        value_head_rows = value_portion.reshape(DOCUMENTS_SHARD, DOCUMENT_ROWS, KEY_VALUE_HEADS, HEAD_WIDTH).astype(jnp.bfloat16)
        grouped_scores = query_head_rows.astype(jnp.float32).reshape(DOCUMENTS_SHARD, DOCUMENT_ROWS, KEY_VALUE_HEADS, heads_per_group, HEAD_WIDTH)
        scores = jnp.einsum('jqhgd,jkhd->jhgqk', grouped_scores, key_head_rows.astype(jnp.float32)) / math.sqrt(HEAD_WIDTH)
        order_range = jnp.arange(DOCUMENT_ROWS)
        causal = order_range[:, None] >= order_range[None, :]
        scores = jnp.where(causal, scores, -jnp.inf)
        row_peak = lax.optimization_barrier(jnp.max(scores, axis=-1, keepdims=True))
        exponent = jnp.exp(scores - row_peak)
        probability = (exponent / lax.optimization_barrier(jnp.sum(exponent, axis=-1, keepdims=True))).astype(jnp.bfloat16)
        blended = jnp.einsum('jhgqk,jkhd->jqhgd', probability.astype(jnp.float32), value_head_rows.astype(jnp.float32))
        keep_row = order_range[None, :] < block_capped[:, None]
        result = jnp.where(keep_row[..., None], blended.reshape(DOCUMENTS_SHARD, DOCUMENT_ROWS, QW), 0.0)
        return result.astype(jnp.bfloat16)
    doc_outputs = lax.map(per_block, (by_doc, capped.reshape(DOCS // DOCUMENTS_SHARD, DOCUMENTS_SHARD)))
    doc_index = jnp.arange(DOCS, dtype=jnp.int32)
    same_dest = dest_shard[None, :] == dest_shard[:, None]
    earlier = doc_index[None, :] < doc_index[:, None]
    slot_rank = lax.optimization_barrier(jnp.sum((same_dest & earlier).astype(jnp.int32), axis=1)).astype(jnp.int32)
    slot = (dest_shard * DOCUMENTS_SHARD + slot_rank).astype(jnp.int32)
    placed = jnp.zeros((DOCS, DOCUMENT_ROWS, QW), jnp.bfloat16).at[slot].set(doc_outputs.reshape(DOCS, DOCUMENT_ROWS, QW))
    return placed.reshape(TOKENS, QW)
```

```python
import math

import jax
import jax.numpy as jnp
from jax import lax
from jax.sharding import PartitionSpec as P

HEAD_WIDTH = 128


rope_base = 500000.0
norm_eps = 1e-05


def rotary_embedding(vectors, token_positions):
    half_width = vectors.shape[-1] // 2
    steps_range = jnp.arange(half_width, dtype=jnp.float32)
    frequency = jnp.exp(steps_range * (-2.0 * math.log(rope_base) / vectors.shape[-1]))
    angles = token_positions[..., None, None] * frequency
    cosine = jnp.cos(angles)
    sine_table = jnp.sin(angles)
    first_half = vectors[..., :half_width]
    second_half = vectors[..., half_width:]
    return jnp.concatenate(
        [
            first_half * cosine - second_half * sine_table,
            second_half * cosine + first_half * sine_table,
        ],
        axis=-1,
    )


def project(source_rows, norm_gain, w_query, w_key, w_value):
    packed_weight = jnp.concatenate([w_query, w_key, w_value], axis=1)
    weight = lax.all_gather(packed_weight, "dp", axis=0, tiled=True)
    gathered = lax.all_gather(source_rows, "tensor", axis=1, tiled=True)
    widened = gathered.astype(jnp.float32)
    row_scale = lax.rsqrt(jnp.mean(widened * widened, axis=1, keepdims=True) + norm_eps)
    normed = (widened * row_scale * norm_gain).astype(jnp.bfloat16)
    return jnp.dot(normed, weight, preferred_element_type=jnp.float32)


def rotate_round(projected, token_positions, rotated_width, head_dim):
    total_rows = projected.shape[0]
    rotated = rotary_embedding(
        projected[:, :rotated_width].reshape(total_rows, -1, head_dim), token_positions
    ).reshape(total_rows, -1)
    return jnp.concatenate([rotated, projected[:, rotated_width:]], axis=1).astype(jnp.bfloat16)


def attend(packed, doc_lengths, query_width, key_width, head_dim, doc_max):
    total_rows = packed.shape[0]
    doc_total = total_rows // doc_max
    value_head_rows = key_width // head_dim
    heads_per_group = query_width // key_width
    queries = packed[:, :query_width].reshape(
        doc_total, doc_max, value_head_rows, heads_per_group, head_dim
    )
    key_rows = packed[:, query_width : query_width + key_width].reshape(
        doc_total, doc_max, value_head_rows, head_dim
    )
    value_rows = packed[:, query_width + key_width :].reshape(
        doc_total, doc_max, value_head_rows, head_dim
    )
    scores = jnp.einsum(
        "jqhgd,jkhd->jhgqk", queries, key_rows, preferred_element_type=jnp.float32
    ) / math.sqrt(head_dim)
    order_range = jnp.arange(doc_max)
    causal = order_range[:, None] >= order_range[None, :]
    scores = jnp.where(causal, scores, -jnp.inf)
    row_peak = jnp.max(scores, axis=-1, keepdims=True)
    exponent = jnp.exp(scores - row_peak)
    probability = (exponent / jnp.sum(exponent, axis=-1, keepdims=True)).astype(jnp.bfloat16)
    blended = jnp.einsum(
        "jhgqk,jkhd->jqhgd", probability, value_rows, preferred_element_type=jnp.float32
    )
    blended = blended.reshape(doc_total, doc_max, query_width)
    row_valid = order_range[None, :] < doc_lengths[:, None]
    result = jnp.where(row_valid[..., None], blended, 0.0)
    return result.reshape(total_rows, query_width).astype(jnp.bfloat16)


def local(
    activations, norm_gain, w_query, w_key, w_value, lengths, languages, lang_caps, dest_shard
):
    shard_count = lax.axis_size("dp")
    my_shard = lax.axis_index("dp")
    doc_count = lengths.shape[0]
    token_rows = activations.shape[0]
    rows_peer = token_rows // doc_count
    doc_max = rows_peer * shard_count
    docs_here = doc_count // shard_count
    head_dim = HEAD_WIDTH
    query_width = w_query.shape[1]
    key_width = w_key.shape[1]
    language_table = jnp.arange(lang_caps.shape[0])
    cap_of_doc = jnp.sum(
        jnp.where(languages[:, None] == language_table[None, :], lang_caps[None, :], 0), axis=1
    )
    capped = jnp.minimum(lengths, cap_of_doc)
    doc_order = jnp.arange(doc_count)
    same_dest = dest_shard[:, None] == dest_shard[None, :]
    doc_rank = jnp.sum(
        (same_dest & (doc_order[None, :] < doc_order[:, None])).astype(jnp.int32), axis=1
    )
    target_slot = dest_shard * docs_here + doc_rank
    holder = jnp.sum(
        jnp.where(doc_order[:, None] == target_slot[None, :], doc_order[None, :], 0), axis=1
    )
    mine = lax.dynamic_slice_in_dim(holder, my_shard * docs_here, docs_here)
    doc_lengths = jnp.take(capped, mine)
    holder_grid = jnp.transpose(holder.reshape(shard_count, docs_here))
    send_index = (
        holder_grid[:, None, :] * rows_peer + jnp.arange(rows_peer)[None, :, None]
    ).reshape(-1)
    token_positions = (
        my_shard + shard_count * (jnp.arange(token_rows) % rows_peer)
    ).astype(jnp.float32)
    projected = project(activations, norm_gain, w_query, w_key, w_value)
    packed = rotate_round(projected, token_positions, query_width + key_width, head_dim)
    outgoing = jnp.take(packed, send_index, axis=0, mode="clip").reshape(
        docs_here, rows_peer, shard_count, -1
    )
    arrived = lax.all_to_all(outgoing, "dp", split_axis=2, concat_axis=2, tiled=True)
    moved_rows = arrived.reshape(docs_here * doc_max, -1)
    return attend(moved_rows, doc_lengths, query_width, key_width, head_dim, doc_max)


def solution(mesh):
    return jax.shard_map(
        local,
        mesh=mesh,
        in_specs=(
            P("dp", "tensor"),
            P(),
            P("dp", "tensor"),
            P("dp", "tensor"),
            P("dp", "tensor"),
            P(),
            P(),
            P(),
            P(),
        ),
        out_specs=P("dp", "tensor"),
        check_vma=False,
    )
```

```python
import functools
import heapq
import math

import jax
import jax.numpy as jnp
from jax import lax
from jax.experimental import pallas as pl
from jax.experimental.pallas import tpu as pltpu
from jax.sharding import PartitionSpec as P

HEAD_WIDTH = 128


rope_base = 500000.0
norm_eps = 1e-05


MESH = pl.DeviceIdType.MESH
LANES = 128
Y_CHIPS, Z_CHIPS, CORES, X_CHIPS = 4, 8, 2, 4
ROW_CHUNKS = 4
LEFT_COLUMNS = 768


def hops_az(s):
    return 4 if s == 1 else 3


def hops_ay(s, dz):
    return 2 if (dz % 2 == 0) == (s == 1) else 1


def hops_by(s):
    return 1 if s == 1 else 2


def hops_bz(s, dy):
    return 4 if (dy % 2 == 0) == (s == 1) else 3


def first_sends():
    sends = [("az", s, 1) for s in (1, -1)] + [("by", s, 1) for s in (1, -1)]
    sends += [("ay", s, 0, 1) for s in (1, -1)] + [("bz", s, 0, 1) for s in (1, -1)]
    return sends + [("xo", s, r) for r in range(2) for s in (1, -1)]


def next_sends(key):
    kind, s = key[:2]
    sends = []
    if kind == "az":
        if key[2] < hops_az(s):
            sends.append(("az", s, key[2] + 1))
        sends += [("ay", q, -s * key[2], 1) for q in (1, -1)]
    elif kind == "ay":
        if key[3] < hops_ay(s, key[2]):
            sends.append(("ay", s, key[2], key[3] + 1))
    elif kind == "by":
        if key[2] < hops_by(s):
            sends.append(("by", s, key[2] + 1))
        sends += [("bz", q, -s * key[2], 1) for q in (1, -1)]
    elif kind == "bz":
        if key[3] < hops_bz(s, key[2]):
            sends.append(("bz", s, key[2], key[3] + 1))
    elif kind == "xo":
        sends.append(("xf", s, key[2]))
        if key[2] + 2 < ROW_CHUNKS:
            sends.append(("xo", s, key[2] + 2))
    return sends


def arrival_order(left, right, row_bytes):
    cost = {"az": left, "ay": left, "by": right, "bz": right, "xo": row_bytes, "xf": row_bytes // 2}
    free, queue, order, count = {}, [], [], 0
    pending = [(0.0, key) for key in first_sends()]
    while pending or queue:
        for now, key in pending:
            link = ({"a": key[0][1], "b": key[0][1], "x": "x"}[key[0][0]], key[1])
            free[link] = max(now, free.get(link, 0.0)) + cost[key[0]] / 46.5e3
            heapq.heappush(queue, (free[link] + 1.6, count, key))
            count += 1
        now, _, key = heapq.heappop(queue)
        order.append(key)
        pending = [(now, k) for k in next_sends(key)]
    return order


def project_kernel(
    order, x_ref, gain_ref, wq_ref, wk_ref, wv_ref, cos_ref, sin_ref, out_ref,
    wa, wb, raw, normed, send_sems, recv_sems, pass_sems, passed_sems, local_sems,
):
    me = lax.axis_index("dp")
    my_x = lax.axis_index("tensor")
    my_y, my_z, my_c = me // (Z_CHIPS * CORES), (me // CORES) % Z_CHIPS, me % CORES
    other_c = 1 - my_c
    rows = raw.shape[1] // ROW_CHUNKS
    features = raw.shape[2]
    shard = wq_ref.shape[0]
    left_w, right_w = wa.shape[1], wb.shape[1]

    def device(dx=0, dy=0, dz=0, core=None):
        y = (my_y + dy + Y_CHIPS) % Y_CHIPS
        z = (my_z + dz + Z_CHIPS) % Z_CHIPS
        core = my_c if core is None else core
        return ((y * Z_CHIPS + z) * CORES + core, (my_x + dx + X_CHIPS) % X_CHIPS)

    neighbours = [
        device(dx=1), device(dx=-1), device(dy=1), device(dy=-1), device(dz=1), device(dz=-1),
        device(core=other_c),
    ]

    def weight_rows(dy, dz, core):
        y = (my_y + dy + 2 * Y_CHIPS) % Y_CHIPS
        z = (my_z + dz + 2 * Z_CHIPS) % Z_CHIPS
        return pl.ds(pl.multiple_of(((core * Y_CHIPS + y) * Z_CHIPS + z) * shard, shard), shard)

    sibling = device(core=other_c)
    names = {key: n for n, key in enumerate(order)}

    def piece(key, back):
        kind, s = key[:2]
        if kind == "az":
            return wa.at[weight_rows(0, -s * back, my_c), :]
        if kind == "ay":
            return wa.at[weight_rows(-s * back, key[2], my_c), :]
        if kind == "by":
            return wb.at[weight_rows(-s * back, 0, my_c), :]
        if kind == "bz":
            return wb.at[weight_rows(key[2], -s * back, my_c), :]
        at = (my_x - s * back + 2 * X_CHIPS) % X_CHIPS
        chunk = pl.ds(key[2] * rows, rows)
        if kind == "xo":
            return raw.at[at, chunk, :]
        half = features // 2
        return raw.at[at, chunk, pl.ds(0 if s == 1 else half, half)]

    def made(key):
        return {"az": key[-1] - 1, "ay": key[-1] - 1, "by": key[-1] - 1, "bz": key[-1] - 1, "xo": 0, "xf": 1}[key[0]]

    def copy(key):
        n = names[key]
        axis = {"a": "d" + key[0][1], "b": "d" + key[0][1], "x": "dx"}[key[0][0]]
        ref = piece(key, made(key))
        return pltpu.make_async_remote_copy(
            src_ref=ref, dst_ref=ref, send_sem=send_sems.at[n], recv_sem=recv_sems.at[n],
            device_id=device(**{axis: key[1]}), device_id_type=MESH,
        )

    def landing(key):
        n = names[key]
        ref = piece(key, made(key) + 1)
        return pltpu.make_async_remote_copy(
            src_ref=ref, dst_ref=ref, send_sem=send_sems.at[n], recv_sem=recv_sems.at[n],
            device_id=sibling, device_id_type=MESH,
        )

    passes = []

    def pass_on(buffer, ref):
        c = pltpu.make_async_remote_copy(
            src_ref=ref, dst_ref=ref, send_sem=pass_sems.at[len(passes)], recv_sem=passed_sems.at[buffer],
            device_id=sibling, device_id_type=MESH,
        )
        c.start()
        passes.append(c)

    own = weight_rows(0, 0, my_c)
    local = [
        pltpu.make_async_copy(wq_ref.at[:, pl.ds(0, left_w)], wa.at[own, :], local_sems.at[0]),
        pltpu.make_async_copy(
            wq_ref.at[:, pl.ds(left_w, right_w - 2 * LANES)],
            wb.at[own, pl.ds(0, right_w - 2 * LANES)], local_sems.at[1],
        ),
        pltpu.make_async_copy(wk_ref, wb.at[own, pl.ds(right_w - 2 * LANES, LANES)], local_sems.at[2]),
        pltpu.make_async_copy(wv_ref, wb.at[own, pl.ds(right_w - LANES, LANES)], local_sems.at[3]),
        pltpu.make_async_copy(x_ref, raw.at[my_x], local_sems.at[4]),
    ]
    for c in local:
        c.start()
    barrier = pltpu.get_barrier_semaphore()
    for n in neighbours:
        pl.semaphore_signal(barrier, inc=1, device_id=n, device_id_type=MESH)
    pl.semaphore_wait(barrier, len(neighbours))
    for c in local:
        c.wait()

    sent = []

    def send(key):
        c = copy(key)
        c.start()
        sent.append(c)

    for key in first_sends():
        send(key)
    pass_on(0, wa.at[own, :])
    pass_on(1, wb.at[own, :])

    def normalise(chunk):
        step = 16

        @pl.loop(0, rows // step)
        def _(i):
            at = pl.ds(pl.multiple_of(chunk * rows + i * step, step), step)
            total = jnp.zeros((step, 1), jnp.float32)
            for q in range(X_CHIPS):
                v = raw[q, at, :].astype(jnp.float32)
                total += jnp.sum(v * v, axis=1, keepdims=True)
            scale = lax.rsqrt(total / (X_CHIPS * features) + norm_eps)
            for q in range(X_CHIPS):
                v = raw[q, at, :].astype(jnp.float32)
                g = gain_ref[:, pl.ds(q * features, features)]
                n = (v * scale * g).astype(jnp.bfloat16)
                for z in range(Z_CHIPS):
                    for c in range(CORES):
                        src = (z * CORES + c) * shard
                        dst = ((c * Y_CHIPS + q) * Z_CHIPS + z) * shard
                        normed[at, pl.ds(dst, shard)] = n[:, src : src + shard]

    halves = {}
    for key in order:
        landing(key).wait_recv()
        for k in next_sends(key):
            send(k)
        kind = key[0]
        if kind[0] == "a":
            pass_on(0, piece(key, made(key) + 1))
        elif kind[0] == "b":
            pass_on(1, piece(key, made(key) + 1))
        elif kind == "xf":
            halves[key[2]] = halves.get(key[2], 0) + 1
            if halves[key[2]] == 2:
                normalise(key[2])

    span = wa.shape[0] // CORES
    theirs = pl.ds(pl.multiple_of(other_c * span, span), span)
    for n, ref in enumerate((wa.at[theirs, :], wb.at[theirs, :])):
        pltpu.make_async_remote_copy(
            src_ref=ref, dst_ref=ref, send_sem=pass_sems.at[0], recv_sem=passed_sems.at[n],
            device_id=sibling, device_id_type=MESH,
        ).wait_recv()

    block_rows, block = 256, 2 * LANES
    head = HEAD_WIDTH
    cosine, sine = cos_ref[...], sin_ref[...]

    def turn(v):
        shaped = v.reshape(block_rows // 8, 8, head)
        turned = pltpu.roll(v, head // 2, 1).reshape(block_rows // 8, 8, head)
        return (shaped * cosine[None] + turned * sine[None]).reshape(block_rows, head)

    @pl.loop(0, normed.shape[0] // block_rows)
    def _(m):
        at = pl.ds(pl.multiple_of(m * block_rows, block_rows), block_rows)

        def product(w, n):
            return jnp.dot(normed[at, :], w[:, pl.ds(n, block)], preferred_element_type=jnp.float32)

        def store(v, column, turned):
            for h in range(2):
                part = v[:, h * head : (h + 1) * head]
                part = turn(part) if turned[h] else part
                out_ref[at, pl.ds(column + h * head, head)] = part.astype(jnp.bfloat16)

        @pl.loop(0, left_w // block)
        def _(n):
            col = pl.multiple_of(n * block, block)
            store(product(wa, col), col, (True, True))

        store(product(wb, 0), left_w, (True, True))
        store(product(wb, block), left_w + block, (True, False))

    for c in sent + passes:
        c.wait_send()


def project(activations, norm_gain, w_query, w_key, w_value, cosine, sine):
    rows, features = activations.shape
    shard = w_query.shape[0]
    columns = w_query.shape[1] + w_key.shape[1] + w_value.shape[1]
    right = columns - LEFT_COLUMNS
    depth = shard * Y_CHIPS * Z_CHIPS * CORES
    order = arrival_order(shard * LEFT_COLUMNS * 2, shard * right * 2, rows // ROW_CHUNKS * features * 2)
    passes = 2 * Y_CHIPS * Z_CHIPS
    vmem = pl.BlockSpec(memory_space=pltpu.VMEM)
    hbm = pl.BlockSpec(memory_space=pl.ANY)
    return pl.pallas_call(
        functools.partial(project_kernel, order),
        out_shape=jax.ShapeDtypeStruct((rows, columns), jnp.bfloat16),
        in_specs=[hbm, vmem, hbm, hbm, hbm, vmem, vmem],
        out_specs=vmem,
        scratch_shapes=[
            pltpu.VMEM((depth, LEFT_COLUMNS), jnp.bfloat16),
            pltpu.VMEM((depth, right), jnp.bfloat16),
            pltpu.VMEM((X_CHIPS, rows, features), jnp.bfloat16),
            pltpu.VMEM((rows, X_CHIPS * features), jnp.bfloat16),
            pltpu.SemaphoreType.DMA((len(order),)),
            pltpu.SemaphoreType.DMA((len(order),)),
            pltpu.SemaphoreType.DMA((passes,)),
            pltpu.SemaphoreType.DMA((2,)),
            pltpu.SemaphoreType.DMA((5,)),
        ],
        compiler_params=pltpu.CompilerParams(
            collective_id=0, has_side_effects=True, vmem_limit_bytes=60 * 1024 * 1024
        ),
        name="project",
    )(activations, norm_gain.reshape(1, -1), w_query, w_key, w_value, cosine, sine)


def rotation_tables(positions, head_dim):
    half_width = head_dim // 2
    steps_range = jnp.arange(half_width, dtype=jnp.float32)
    frequency = jnp.exp(steps_range * (-2.0 * math.log(rope_base) / head_dim))
    angles = positions[:, None] * frequency
    cosine, sine = jnp.cos(angles), jnp.sin(angles)
    return jnp.concatenate([cosine, cosine], axis=1), jnp.concatenate([-sine, sine], axis=1)


def attend(packed, doc_lengths, query_width, key_width, head_dim, doc_max):
    total_rows = packed.shape[0]
    doc_total = total_rows // doc_max
    value_head_rows = key_width // head_dim
    heads_per_group = query_width // key_width
    queries = packed[:, :query_width].reshape(
        doc_total, doc_max, value_head_rows, heads_per_group, head_dim
    )
    key_rows = packed[:, query_width : query_width + key_width].reshape(
        doc_total, doc_max, value_head_rows, head_dim
    )
    value_rows = packed[:, query_width + key_width :].reshape(
        doc_total, doc_max, value_head_rows, head_dim
    )
    scores = jnp.einsum(
        "jqhgd,jkhd->jhgqk", queries, key_rows, preferred_element_type=jnp.float32
    ) / math.sqrt(head_dim)
    order_range = jnp.arange(doc_max)
    causal = order_range[:, None] >= order_range[None, :]
    scores = jnp.where(causal, scores, -jnp.inf)
    row_peak = jnp.max(scores, axis=-1, keepdims=True)
    exponent = jnp.exp(scores - row_peak)
    probability = (exponent / jnp.sum(exponent, axis=-1, keepdims=True)).astype(jnp.bfloat16)
    blended = jnp.einsum(
        "jhgqk,jkhd->jqhgd", probability, value_rows, preferred_element_type=jnp.float32
    )
    blended = blended.reshape(doc_total, doc_max, query_width)
    row_valid = order_range[None, :] < doc_lengths[:, None]
    result = jnp.where(row_valid[..., None], blended, 0.0)
    return result.reshape(total_rows, query_width).astype(jnp.bfloat16)


def local(
    activations, norm_gain, w_query, w_key, w_value, lengths, languages, lang_caps, dest_shard
):
    shard_count = lax.axis_size("dp")
    my_shard = lax.axis_index("dp")
    doc_count = lengths.shape[0]
    token_rows = activations.shape[0]
    rows_peer = token_rows // doc_count
    doc_max = rows_peer * shard_count
    docs_here = doc_count // shard_count
    head_dim = HEAD_WIDTH
    query_width = w_query.shape[1]
    key_width = w_key.shape[1]
    language_table = jnp.arange(lang_caps.shape[0])
    cap_of_doc = jnp.sum(
        jnp.where(languages[:, None] == language_table[None, :], lang_caps[None, :], 0), axis=1
    )
    capped = jnp.minimum(lengths, cap_of_doc)
    doc_order = jnp.arange(doc_count)
    same_dest = dest_shard[:, None] == dest_shard[None, :]
    doc_rank = jnp.sum(
        (same_dest & (doc_order[None, :] < doc_order[:, None])).astype(jnp.int32), axis=1
    )
    target_slot = dest_shard * docs_here + doc_rank
    holder = jnp.sum(
        jnp.where(doc_order[:, None] == target_slot[None, :], doc_order[None, :], 0), axis=1
    )
    mine = lax.dynamic_slice_in_dim(holder, my_shard * docs_here, docs_here)
    doc_lengths = jnp.take(capped, mine)
    holder_grid = jnp.transpose(holder.reshape(shard_count, docs_here))
    send_index = (
        holder_grid[:, None, :] * rows_peer + jnp.arange(rows_peer)[None, :, None]
    ).reshape(-1)
    positions = (my_shard + shard_count * (jnp.arange(8) % rows_peer)).astype(jnp.float32)
    cosine, sine = rotation_tables(positions, head_dim)
    packed = project(activations, norm_gain, w_query, w_key, w_value, cosine, sine)
    outgoing = jnp.take(packed, send_index, axis=0, mode="clip").reshape(
        docs_here, rows_peer, shard_count, -1
    )
    arrived = lax.all_to_all(outgoing, "dp", split_axis=2, concat_axis=2, tiled=True)
    moved_rows = arrived.reshape(docs_here * doc_max, -1)
    return attend(moved_rows, doc_lengths, query_width, key_width, head_dim, doc_max)


def solution(mesh):
    return jax.shard_map(
        local,
        mesh=mesh,
        in_specs=(
            P("dp", "tensor"),
            P(),
            P("dp", "tensor"),
            P("dp", "tensor"),
            P("dp", "tensor"),
            P(),
            P(),
            P(),
            P(),
        ),
        out_specs=P("dp", "tensor"),
        check_vma=False,
    )
```

```python
import functools
import heapq
import math

import jax
import jax.numpy as jnp
from jax import lax
from jax.experimental import pallas as pl
from jax.experimental.pallas import tpu as pltpu
from jax.sharding import PartitionSpec as P

HEAD_WIDTH = 128


rope_base = 500000.0
norm_eps = 1e-05


MESH = pl.DeviceIdType.MESH
LANES = 128
Y_CHIPS, Z_CHIPS, CORES, X_CHIPS = 4, 8, 2, 4
ROW_CHUNKS = 4
CHUNK_DY = (2, 1, 3, 0)
SEND_DZ = (4, 3, 5, 2, 6, 1, 7, 0)
LEFT_COLUMNS = 768


def hops_az(s):
    return 4 if s == 1 else 3


def hops_ay(s, dz):
    return 2 if (dz % 2 == 0) == (s == 1) else 1


def hops_by(s):
    return 1 if s == 1 else 2


def hops_bz(s, dy):
    return 4 if (dy % 2 == 0) == (s == 1) else 3


def first_sends():
    sends = [("az", s, 1) for s in (1, -1)] + [("by", s, 1) for s in (1, -1)]
    return sends + [("ay", s, 0, 1) for s in (1, -1)] + [("bz", s, 0, 1) for s in (1, -1)]


def first_rows(chunk):
    return [("xo", s, chunk) for s in (1, -1)]


def next_sends(key):
    kind, s = key[:2]
    sends = []
    if kind == "az":
        if key[2] < hops_az(s):
            sends.append(("az", s, key[2] + 1))
        sends += [("ay", q, -s * key[2], 1) for q in (1, -1)]
    elif kind == "ay":
        if key[3] < hops_ay(s, key[2]):
            sends.append(("ay", s, key[2], key[3] + 1))
    elif kind == "by":
        if key[2] < hops_by(s):
            sends.append(("by", s, key[2] + 1))
        sends += [("bz", q, -s * key[2], 1) for q in (1, -1)]
    elif kind == "bz":
        if key[3] < hops_bz(s, key[2]):
            sends.append(("bz", s, key[2], key[3] + 1))
    elif kind == "xo":
        sends.append(("xf", s, key[2]))
        if key[2] + 2 < ROW_CHUNKS:
            sends.append(("xo", s, key[2] + 2))
    return sends


def arrival_order(left, right, row_bytes):
    cost = {"az": left, "ay": left, "by": right, "bz": right, "xo": row_bytes, "xf": row_bytes // 2}
    free, queue, order, count = {}, [], [], 0
    pending = [(0.0, key) for key in first_sends() + first_rows(0) + first_rows(1)]
    while pending or queue:
        for now, key in pending:
            link = ({"a": key[0][1], "b": key[0][1], "x": "x"}[key[0][0]], key[1])
            free[link] = max(now, free.get(link, 0.0)) + cost[key[0]] / 46.5e3
            heapq.heappush(queue, (free[link] + 1.6, count, key))
            count += 1
        now, _, key = heapq.heappop(queue)
        order.append(key)
        pending = [(now, k) for k in next_sends(key)]
    return order


def project_kernel(
    order, x_ref, place_ref, gain_ref, wq_ref, wk_ref, wv_ref, cos_ref, sin_ref, arrived,
    wa, wb, mine, raw, normed, packed,
    send_sems, recv_sems, pass_sems, passed_sems, local_sems, out_sems, in_sem,
):
    me = lax.axis_index("dp")
    my_x = lax.axis_index("tensor")
    my_y, my_z, my_c = me // (Z_CHIPS * CORES), (me // CORES) % Z_CHIPS, me % CORES
    other_c = 1 - my_c
    rows = raw.shape[1] // ROW_CHUNKS
    features = raw.shape[2]
    shard = wq_ref.shape[0]
    left_w, right_w = wa.shape[1], wb.shape[1]

    def device(dx=0, dy=0, dz=0, core=None):
        y = (my_y + dy + Y_CHIPS) % Y_CHIPS
        z = (my_z + dz + Z_CHIPS) % Z_CHIPS
        core = my_c if core is None else core
        return ((y * Z_CHIPS + z) * CORES + core, (my_x + dx + X_CHIPS) % X_CHIPS)

    neighbours = [
        device(dx=1), device(dx=-1), device(dy=1), device(dy=-1), device(dz=1), device(dz=-1),
        device(core=other_c),
    ]

    def weight_rows(dy, dz, core):
        y = (my_y + dy + 2 * Y_CHIPS) % Y_CHIPS
        z = (my_z + dz + 2 * Z_CHIPS) % Z_CHIPS
        return pl.ds(pl.multiple_of(((core * Y_CHIPS + y) * Z_CHIPS + z) * shard, shard), shard)

    sibling = device(core=other_c)
    names = {key: n for n, key in enumerate(order)}

    def piece(key, back):
        kind, s = key[:2]
        if kind == "az":
            return wa.at[weight_rows(0, -s * back, my_c), :]
        if kind == "ay":
            return wa.at[weight_rows(-s * back, key[2], my_c), :]
        if kind == "by":
            return wb.at[weight_rows(-s * back, 0, my_c), :]
        if kind == "bz":
            return wb.at[weight_rows(key[2], -s * back, my_c), :]
        at = (my_x - s * back + 2 * X_CHIPS) % X_CHIPS
        chunk = pl.ds(key[2] * rows, rows)
        if kind == "xo":
            return raw.at[at, chunk, :]
        half = features // 2
        return raw.at[at, chunk, pl.ds(0 if s == 1 else half, half)]

    def made(key):
        return {"az": key[-1] - 1, "ay": key[-1] - 1, "by": key[-1] - 1, "bz": key[-1] - 1, "xo": 0, "xf": 1}[key[0]]

    def copy(key):
        n = names[key]
        axis = {"a": "d" + key[0][1], "b": "d" + key[0][1], "x": "dx"}[key[0][0]]
        ref = piece(key, made(key))
        return pltpu.make_async_remote_copy(
            src_ref=ref, dst_ref=ref, send_sem=send_sems.at[n], recv_sem=recv_sems.at[n],
            device_id=device(**{axis: key[1]}), device_id_type=MESH,
        )

    def landing(key):
        n = names[key]
        ref = piece(key, made(key) + 1)
        return pltpu.make_async_remote_copy(
            src_ref=ref, dst_ref=ref, send_sem=send_sems.at[n], recv_sem=recv_sems.at[n],
            device_id=sibling, device_id_type=MESH,
        )

    passes = []

    def pass_on(buffer, ref):
        c = pltpu.make_async_remote_copy(
            src_ref=ref, dst_ref=ref, send_sem=pass_sems.at[len(passes)], recv_sem=passed_sems.at[buffer],
            device_id=sibling, device_id_type=MESH,
        )
        c.start()
        passes.append(c)

    own = weight_rows(0, 0, my_c)
    local = [
        pltpu.make_async_copy(wq_ref.at[:, pl.ds(0, left_w)], wa.at[own, :], local_sems.at[0]),
        pltpu.make_async_copy(
            wq_ref.at[:, pl.ds(left_w, right_w - 2 * LANES)],
            wb.at[own, pl.ds(0, right_w - 2 * LANES)], local_sems.at[1],
        ),
        pltpu.make_async_copy(wk_ref, wb.at[own, pl.ds(right_w - 2 * LANES, LANES)], local_sems.at[2]),
        pltpu.make_async_copy(wv_ref, wb.at[own, pl.ds(right_w - LANES, LANES)], local_sems.at[3]),
        pltpu.make_async_copy(x_ref, mine, local_sems.at[4]),
    ]
    for c in local:
        c.start()
    barrier = pltpu.get_barrier_semaphore()
    for n in neighbours:
        pl.semaphore_signal(barrier, inc=1, device_id=n, device_id_type=MESH)
    pl.semaphore_wait(barrier, len(neighbours))
    for c in local[:4]:
        c.wait()

    sent = []

    def send(key):
        c = copy(key)
        c.start()
        sent.append(c)

    for key in first_sends():
        send(key)
    pass_on(0, wa.at[own, :])
    pass_on(1, wb.at[own, :])

    def order_rows(chunk):
        p = lax.broadcasted_iota(jnp.int32, (rows, raw.shape[1]), 0)
        y = (my_y + CHUNK_DY[chunk]) % Y_CHIPS
        z = (my_z + (p >> 4)) & (Z_CHIPS - 1)
        c = (my_c + (p >> 3)) & (CORES - 1)
        wanted = ((y * Z_CHIPS + z) * CORES + c) * 8 + (p & 7)
        pick = jnp.where(wanted == place_ref[...], 1.0, 0.0).astype(jnp.bfloat16)
        width = 512
        for n in range(0, features, width):
            picked = jnp.dot(pick, mine[:, pl.ds(n, width)], preferred_element_type=jnp.float32)
            raw[my_x, pl.ds(chunk * rows, rows), pl.ds(n, width)] = picked.astype(jnp.bfloat16)

    local[4].wait()
    for chunk in range(ROW_CHUNKS):
        order_rows(chunk)
        if chunk < 2:
            for key in first_rows(chunk):
                send(key)

    def normalise(chunk):
        step = 16

        @pl.loop(0, rows // step)
        def _(i):
            at = pl.ds(pl.multiple_of(chunk * rows + i * step, step), step)
            total = jnp.zeros((step, 1), jnp.float32)
            for q in range(X_CHIPS):
                v = raw[q, at, :].astype(jnp.float32)
                total += jnp.sum(v * v, axis=1, keepdims=True)
            scale = lax.rsqrt(total / (X_CHIPS * features) + norm_eps)
            for q in range(X_CHIPS):
                v = raw[q, at, :].astype(jnp.float32)
                g = gain_ref[:, pl.ds(q * features, features)]
                n = (v * scale * g).astype(jnp.bfloat16)
                for z in range(Z_CHIPS):
                    for c in range(CORES):
                        src = (z * CORES + c) * shard
                        dst = ((c * Y_CHIPS + q) * Z_CHIPS + z) * shard
                        normed[at, pl.ds(dst, shard)] = n[:, src : src + shard]

    block_rows, block = 2 * rows, 2 * LANES
    head = HEAD_WIDTH
    cosine, sine = cos_ref[...], sin_ref[...]

    def turn(v):
        turned = pltpu.roll(v, head // 2, 1).reshape(block_rows // 8, 8, head)
        return v.reshape(block_rows // 8, 8, head) * cosine[None] + turned * sine[None]

    def multiply(m):
        at = pl.ds(m * block_rows, block_rows)
        groups = pl.ds(m * block_rows // 8, block_rows // 8)

        def product(w, n):
            return jnp.dot(normed[at, :], w[:, pl.ds(n, block)], preferred_element_type=jnp.float32)

        def store(v, column, turned):
            for h in range(2):
                part = v[:, h * head : (h + 1) * head]
                part = turn(part) if turned[h] else part.reshape(block_rows // 8, 8, head)
                packed[groups, :, pl.ds(column + h * head, head)] = part.astype(jnp.bfloat16)

        @pl.loop(0, left_w // block)
        def _(n):
            col = pl.multiple_of(n * block, block)
            store(product(wa, col), col, (True, True))

        store(product(wb, 0), left_w, (True, True))
        store(product(wb, block), left_w + block, (True, False))

    outgoing = []

    def hand_out(chunk):
        for dz in SEND_DZ:
            for dc in range(CORES):
                group = (chunk * Z_CHIPS + dz) * CORES + dc
                core = other_c if dc else my_c
                if CHUNK_DY[chunk] or dz or dc:
                    c = pltpu.make_async_remote_copy(
                        src_ref=packed.at[group], dst_ref=arrived.at[me], send_sem=out_sems.at[group], recv_sem=in_sem,
                        device_id=device(dy=CHUNK_DY[chunk], dz=dz, core=core), device_id_type=MESH,
                    )
                    outgoing.append(c)
                else:
                    c = pltpu.make_async_copy(packed.at[group], arrived.at[me], out_sems.at[group])
                    own_group.append(c)
                c.start()

    own_group = []
    halves = {}
    left = sum(key[0][0] != "x" for key in order)
    span = wa.shape[0] // CORES
    theirs = pl.ds(pl.multiple_of(other_c * span, span), span)
    for key in order:
        landing(key).wait_recv()
        for k in next_sends(key):
            send(k)
        kind = key[0]
        if kind[0] == "a":
            pass_on(0, piece(key, made(key) + 1))
        elif kind[0] == "b":
            pass_on(1, piece(key, made(key) + 1))
        elif kind == "xf":
            halves[key[2]] = halves.get(key[2], 0) + 1
            if halves[key[2]] == 2:
                normalise(key[2])
        left -= kind[0] != "x"
        if kind[0] != "x" and left == 0:
            for n, ref in enumerate((wa.at[theirs, :], wb.at[theirs, :])):
                pltpu.make_async_remote_copy(
                    src_ref=ref, dst_ref=ref, send_sem=pass_sems.at[0], recv_sem=passed_sems.at[n],
                    device_id=sibling, device_id_type=MESH,
                ).wait_recv()
            assert halves[0] == halves[1] == 2
            multiply(0)
            hand_out(0)
            hand_out(1)
    multiply(1)
    hand_out(2)
    hand_out(3)

    for c in sent + passes + outgoing:
        c.wait_send()
    own_group[0].wait()
    groups = arrived.at[pl.ds(0, len(outgoing))]
    pltpu.make_async_remote_copy(
        src_ref=groups, dst_ref=groups, send_sem=out_sems.at[0], recv_sem=in_sem,
        device_id=sibling, device_id_type=MESH,
    ).wait_recv()


def project(activations, place, norm_gain, w_query, w_key, w_value, cosine, sine):
    rows, features = activations.shape
    shard = w_query.shape[0]
    columns = w_query.shape[1] + w_key.shape[1] + w_value.shape[1]
    right = columns - LEFT_COLUMNS
    depth = shard * Y_CHIPS * Z_CHIPS * CORES
    order = arrival_order(shard * LEFT_COLUMNS * 2, shard * right * 2, rows // ROW_CHUNKS * features * 2)
    passes = 2 * Y_CHIPS * Z_CHIPS
    vmem = pl.BlockSpec(memory_space=pltpu.VMEM)
    hbm = pl.BlockSpec(memory_space=pl.ANY)
    return pl.pallas_call(
        functools.partial(project_kernel, order),
        out_shape=jax.ShapeDtypeStruct((rows // 8, 8, columns), jnp.bfloat16),
        in_specs=[hbm, vmem, vmem, hbm, hbm, hbm, vmem, vmem],
        out_specs=hbm,
        scratch_shapes=[
            pltpu.VMEM((depth, LEFT_COLUMNS), jnp.bfloat16),
            pltpu.VMEM((depth, right), jnp.bfloat16),
            pltpu.VMEM((rows, features), jnp.bfloat16),
            pltpu.VMEM((X_CHIPS, rows, features), jnp.bfloat16),
            pltpu.VMEM((rows, X_CHIPS * features), jnp.bfloat16),
            pltpu.VMEM((rows // 8, 8, columns), jnp.bfloat16),
            pltpu.SemaphoreType.DMA((len(order),)),
            pltpu.SemaphoreType.DMA((len(order),)),
            pltpu.SemaphoreType.DMA((passes,)),
            pltpu.SemaphoreType.DMA((2,)),
            pltpu.SemaphoreType.DMA((5,)),
            pltpu.SemaphoreType.DMA((rows // 8,)),
            pltpu.SemaphoreType.DMA,
        ],
        compiler_params=pltpu.CompilerParams(
            collective_id=0, has_side_effects=True, vmem_limit_bytes=60 * 1024 * 1024
        ),
        name="project",
    )(activations, place, norm_gain.reshape(1, -1), w_query, w_key, w_value, cosine, sine)


def rotation_tables(positions, head_dim):
    half_width = head_dim // 2
    steps_range = jnp.arange(half_width, dtype=jnp.float32)
    frequency = jnp.exp(steps_range * (-2.0 * math.log(rope_base) / head_dim))
    angles = positions[:, None] * frequency
    cosine, sine = jnp.cos(angles), jnp.sin(angles)
    return jnp.concatenate([cosine, cosine], axis=1), jnp.concatenate([-sine, sine], axis=1)


def attend_kernel(lengths_ref, rows_ref, out_ref, ordered, *, query_width, head, docs):
    total = rows_ref.shape[0]
    doc_rows = total // docs
    shards = total // 8
    per_doc = 8 // docs
    s = lax.broadcasted_iota(jnp.int32, (total, total), 0)
    i = lax.broadcasted_iota(jnp.int32, (total, total), 1)
    source = (s % shards) * 8 + (s // doc_rows) * per_doc + (s // shards) % per_doc
    pick = jnp.where(i == source, 1.0, 0.0).astype(jnp.bfloat16)
    ordered[...] = jnp.dot(pick, rows_ref[...], preferred_element_type=jnp.float32).astype(jnp.bfloat16)
    a = lax.broadcasted_iota(jnp.int32, (doc_rows, doc_rows), 0)
    b = lax.broadcasted_iota(jnp.int32, (doc_rows, doc_rows), 1)
    t = lax.broadcasted_iota(jnp.int32, (doc_rows, head), 0)
    for doc in range(docs):
        at = pl.ds(doc * doc_rows, doc_rows)
        key = ordered[at, pl.ds(query_width, head)]
        value = ordered[at, pl.ds(query_width + head, head)]
        kept = t < lengths_ref[doc]
        for n in range(query_width // head):
            query = ordered[at, pl.ds(n * head, head)]
            score = lax.dot_general(
                query, key, (((1,), (1,)), ((), ())), preferred_element_type=jnp.float32
            ) / math.sqrt(head)
            score = jnp.where(a >= b, score, -jnp.inf)
            exponent = jnp.exp(score - jnp.max(score, axis=1, keepdims=True))
            probs = (exponent / jnp.sum(exponent, axis=1, keepdims=True)).astype(jnp.bfloat16)
            blended = jnp.dot(probs, value, preferred_element_type=jnp.float32)
            out_ref[at, pl.ds(n * head, head)] = jnp.where(kept, blended, 0.0).astype(jnp.bfloat16)


def attend(rows, doc_lengths, query_width, head):
    total, columns = rows.shape
    vmem = pl.BlockSpec(memory_space=pltpu.VMEM)
    return pl.pallas_call(
        functools.partial(attend_kernel, query_width=query_width, head=head, docs=doc_lengths.shape[0]),
        out_shape=jax.ShapeDtypeStruct((total, query_width), jnp.bfloat16),
        in_specs=[pl.BlockSpec(memory_space=pltpu.SMEM), vmem],
        out_specs=vmem,
        scratch_shapes=[pltpu.VMEM((total, columns), jnp.bfloat16)],
        name="attend",
    )(doc_lengths, rows)


def local(
    activations, norm_gain, w_query, w_key, w_value, lengths, languages, lang_caps, dest_shard
):
    shard_count = lax.axis_size("dp")
    my_shard = lax.axis_index("dp")
    doc_count = lengths.shape[0]
    token_rows = activations.shape[0]
    rows_peer = token_rows // doc_count
    docs_here = doc_count // shard_count
    query_width = w_query.shape[1]
    doc_order = jnp.arange(doc_count)
    earlier = (dest_shard[:, None] == dest_shard[None, :]) & (doc_order[:, None] < doc_order[None, :])
    doc_rank = jnp.sum(earlier.astype(jnp.int32), axis=0)
    slot = dest_shard * docs_here + doc_rank
    place = (slot[:, None] * rows_peer + jnp.arange(rows_peer)[None, :]).reshape(1, -1)
    language_table = jnp.arange(lang_caps.shape[0])
    cap_of_doc = jnp.sum(
        jnp.where(languages[None, :] == language_table[:, None], lang_caps[:, None], 0), axis=0
    )
    capped = jnp.minimum(lengths, cap_of_doc)
    mine = my_shard * docs_here + jnp.arange(docs_here)
    doc_lengths = jnp.sum(jnp.where(slot[None, :] == mine[:, None], capped[None, :], 0), axis=1)
    positions = (my_shard + shard_count * (jnp.arange(8) % rows_peer)).astype(jnp.float32)
    cosine, sine = rotation_tables(positions, HEAD_WIDTH)
    arrived = project(activations, place, norm_gain, w_query, w_key, w_value, cosine, sine)
    return attend(arrived.reshape(token_rows, -1), doc_lengths, query_width, HEAD_WIDTH)


def solution(mesh):
    return jax.shard_map(
        local,
        mesh=mesh,
        in_specs=(
            P("dp", "tensor"),
            P(),
            P("dp", "tensor"),
            P("dp", "tensor"),
            P("dp", "tensor"),
            P(),
            P(),
            P(),
            P(),
        ),
        out_specs=P("dp", "tensor"),
        check_vma=False,
    )
```
